32 devices in a mesh: dp: 8 (over z, x), tensor: 4 (over y, core).
Axes of the slice: x: 2, y: 2, z: 4, core: 2. Of those that a mesh axis runs over, the one named last changes fastest.
Arguments:
- inputs: bfloat16 [16, 512, 2048], P('dp', 'tensor'), may hold values from -6 to 6
- query_weight: bfloat16 [2048, 2048], P('dp', 'tensor'), may hold values from -0.125 to 0.125
- key_weight: bfloat16 [2048, 2048], P('dp', 'tensor'), may hold values from -0.125 to 0.125
- value_weight: bfloat16 [2048, 2048], P('dp', 'tensor'), may hold values from -0.125 to 0.125
- out_weight: bfloat16 [2048, 2048], P('dp', 'tensor'), may hold values from -0.125 to 0.125
- query_gain: float32 [2048], P('tensor'), may hold values from 0.25 to 1.75
- key_gain: float32 [2048], P('tensor'), may hold values from 0.25 to 1.75
- attn_gain: float32 [2048], replicated, may hold values from 0.25 to 1.75
- gate_weight: bfloat16 [2048, 8192], P('dp', 'tensor'), may hold values from -0.125 to 0.125
- up_weight: bfloat16 [2048, 8192], P('dp', 'tensor'), may hold values from -0.125 to 0.125
- down_weight: bfloat16 [2048, 8192], P('dp', 'tensor'), may hold values from -0.0625 to 0.0625
- ffn_gain: float32 [2048], replicated, may hold values from 0.25 to 1.75
- positions: int32 [16, 512], P('dp'), may hold values from 0 to 1023, as said below
- block_ids: int32 [16, 512], P('dp'), may hold values from 0 to 3, never falling along the last dimension, each value on 1 to 256 neighbouring positions
- cotangent: float32 [16, 512, 2048], P('dp', 'tensor'), may hold values from -6 to 6
Outputs:
- output: bfloat16 [16, 512, 2048], P('dp', 'tensor')
- input_grad: float32 [16, 512, 2048], P('dp', 'tensor')
- query_grad: float32 [2048, 2048], P('dp', 'tensor')
- key_grad: float32 [2048, 2048], P('dp', 'tensor')
- value_grad: float32 [2048, 2048], P('dp', 'tensor')
- out_grad: float32 [2048, 2048], P('dp', 'tensor')
- query_gain_grad: float32 [2048], P('tensor')
- key_gain_grad: float32 [2048], P('tensor')
- attn_gain_grad: float32 [2048], replicated
- gate_grad: float32 [2048, 8192], P('dp', 'tensor')
- up_grad: float32 [2048, 8192], P('dp', 'tensor')
- down_grad: float32 [2048, 8192], P('dp', 'tensor')
- ffn_gain_grad: float32 [2048], replicated
The draws below stay inside these ranges and needn't reach their ends.
Inputs may be any that keep to these rules, and one draw needn't show every extreme that they name: `positions`: positions rise strictly along each sequence; the first is 0 and the last 1023. `block_ids`: block ids never fall along a sequence and a block holds at most 256 positions.
All inputs are finite; a program needn't handle non-finite values.
Results may differ from the reference program's by a relative error of at most 0.02.
Values may be sent and summed in bfloat16 or wider, within the bound.
A program may use at most 256 MiB of HBM per device.

```python
import math
import jax
import jax.numpy as jnp
import numpy as np
from jax import lax

D = 2048
HEADS = 16
HD = 128
FF = 8192
LEN = 512
BLOCK = 256
SEQS = 16
SPANS = 4


def draw_positions(key, part):
    row_keys = jax.random.split(key, SEQS)

    def one_row(row_key):
        picked = jax.random.permutation(row_key, 2 * LEN - 2)[:LEN - 2] + 1
        picked = jnp.sort(picked).astype(jnp.int32)
        return jnp.concatenate([jnp.zeros((1,), jnp.int32), picked, jnp.full((1,), 2 * LEN - 1, jnp.int32)])
    return jax.vmap(one_row)(row_keys)


def shard_levels(rng, dims, pieces, smallest, largest):
    factor_of, own = 1.0, jax.random.fold_in(rng, 6)
    for position, shards_of in pieces:
        steps = jnp.exp(jax.random.uniform(jax.random.fold_in(own, position), (shards_of,), jnp.float32, smallest / len(pieces), largest / len(pieces)))
        factor_of = factor_of * jnp.repeat(steps, dims[position] // shards_of).reshape([-1 if axis == position else 1 for axis in range(len(dims))])
    return factor_of


def length_profile(amount, total, most, skew):
    loads = [(1 << 20) // math.isqrt(standing ** skew) + 1 for standing in range(2, amount + 1)]
    surplus, given = total - most - (amount - 1), [1] * (amount - 1)
    while surplus > 0:
        candidates = [i for i in range(amount - 1) if given[i] < most]
        whole, left = sum([loads[i] for i in candidates]), surplus
        for i in candidates:
            addition = min(most - given[i], max(1, left * loads[i] // whole), surplus)
            given[i] = given[i] + addition
            surplus = surplus - addition
    return np.array([most] + given)


def uneven(own_key, number_of, total, most, skew):
    if number_of == 2:
        one = jax.random.randint(own_key, (), max(1, total - most), min(most, total - 1) + 1)
        return jnp.stack([one, total - one])
    lengths = jnp.asarray(length_profile(number_of, total, most, skew), jnp.int32)
    twos = (number_of - 1) // 2
    source_of, sink = lengths[1:1 + 2 * twos:2], lengths[2:2 + 2 * twos:2]
    room = jnp.minimum(source_of - 1, most - sink)
    passed = jax.random.randint(jax.random.fold_in(own_key, 1), (twos,), 0, 1 << 20) % (room + 1)
    lengths = lengths.at[1:1 + 2 * twos:2].set(source_of - passed).at[2:2 + 2 * twos:2].set(sink + passed)
    return lengths[jax.random.permutation(jax.random.fold_in(own_key, 2), number_of)]


def centred(stream_key, dims, width, limit, cuts=(), held_as=jnp.bfloat16):
    factor_of = shard_levels(stream_key, dims, cuts, -0.22, 0.18) if cuts else 1.0
    array = jax.random.normal(stream_key, dims, jnp.float32) * width * factor_of
    return jnp.minimum(jnp.maximum(array, -limit), limit).astype(held_as)


def setup_inputs(seed: int = 0) -> dict:
    key_list = jax.random.split(jax.random.key(seed), 16)
    return {
        "inputs": centred(key_list[0], (SEQS, LEN, D), 1.0, 6.0, ((0, 8), (1, 4))),
        "query_weight": centred(key_list[1], (D, D), D ** -0.5, 0.125, ((0, 8), (1, 4))),
        "key_weight": centred(key_list[2], (D, D), D ** -0.5, 0.125, ((0, 8), (1, 4))),
        "value_weight": centred(key_list[3], (D, D), D ** -0.5, 0.125, ((0, 8), (1, 4))),
        "out_weight": centred(key_list[4], (D, D), D ** -0.5, 0.125, ((0, 8), (1, 4))),
        "query_gain": jnp.clip(1.0 + 0.15 * jax.random.normal(key_list[5], (D,), jnp.float32), 0.25, 1.75),
        "key_gain": jnp.clip(1.0 + 0.15 * jax.random.normal(key_list[6], (D,), jnp.float32), 0.25, 1.75),
        "attn_gain": jnp.clip(1.0 + 0.15 * jax.random.normal(key_list[7], (D,), jnp.float32), 0.25, 1.75),
        "gate_weight": centred(key_list[8], (D, FF), D ** -0.5, 0.125, ((0, 8), (1, 4))),
        "up_weight": centred(key_list[9], (D, FF), D ** -0.5, 0.125, ((0, 8), (1, 4))),
        "down_weight": centred(key_list[10], (D, FF), FF ** -0.5, 0.0625, ((0, 8), (1, 4))),
        "ffn_gain": jnp.clip(1.0 + 0.15 * jax.random.normal(key_list[11], (D,), jnp.float32), 0.25, 1.75),
        "positions": draw_positions(jax.random.fold_in(key_list[15], 71), 0),
        "block_ids": jax.vmap(lambda own: jnp.searchsorted(jnp.cumsum(uneven(own, SPANS, LEN, BLOCK, 0)), jnp.arange(LEN), side="right"))(jax.random.split(key_list[13], SEQS)).reshape((SEQS, LEN)).astype(jnp.int32),
        "cotangent": centred(key_list[14], (SEQS, LEN, D), 1.0, 6.0, ((0, 8), (1, 4)), jnp.float32),
    }


EPS = 1e-06
THETA = 500000.0
HIGH = lax.Precision.HIGHEST

@jax.custom_vjp
def low(v):
    return lax.optimization_barrier(v.astype(jnp.bfloat16)).astype(jnp.float32)

@jax.custom_vjp
def low_back(v):
    return v

def low_keep(v):
    return (low(v), None)

def low_pass(kept, grad):
    return (grad,)

def back_keep(v):
    return (v, None)

def back_low(kept, grad):
    return (low(grad),)
low.defvjp(low_keep, low_pass)
low_back.defvjp(back_keep, back_low)

def product(left, right):
    return jnp.dot(left, right, precision=HIGH)

def post_norm(source, gain_vec):
    return source * lax.rsqrt(lax.optimization_barrier(jnp.mean(source * source, axis=-1, keepdims=True)) + EPS) * gain_vec

def rope_tables(position_ids):
    inv_freq = 1.0 / THETA ** (jnp.arange(0, HD, 2, dtype=jnp.float32) / HD)
    angles = position_ids.astype(jnp.float32)[:, None] * inv_freq[None, :]
    angles = jnp.concatenate([angles, angles], axis=1)
    return (jnp.cos(angles), jnp.sin(angles))

def turn_heads(values, cosine, sine):
    half_width = values.shape[-1] // 2
    rotated = jnp.concatenate([-values[..., half_width:], values[..., :half_width]], axis=-1)
    return values * cosine[:, None, :] + rotated * sine[:, None, :]

def layer(tokens, params, cosine, sine, allowed):
    query_w, key_w, value_w, out_w, query_g, key_g, attn_g, gate_w, up_w, down_w, ffn_g = params
    seq_len = tokens.shape[0]
    query_pre = low_back(product(tokens, query_w))
    key_pre = low_back(product(tokens, key_w))
    value_low = low_back(low(product(tokens, value_w)))
    query_rot = low(turn_heads(post_norm(query_pre, query_g).reshape(seq_len, HEADS, HD), cosine, sine))
    key_rot = low(turn_heads(post_norm(key_pre, key_g).reshape(seq_len, HEADS, HD), cosine, sine))
    scores = low_back(jnp.einsum('qhd,khd->hqk', query_rot, key_rot, precision=HIGH) * HD ** (-0.5))
    scores = jnp.where(allowed[None], scores, -1e+30)
    probs = low(jax.nn.softmax(scores, axis=-1))
    attended = jnp.einsum('hqk,khd->qhd', probs, value_low.reshape(seq_len, HEADS, HD), precision=HIGH)
    attended = low_back(low(attended.reshape(seq_len, D)))
    branch = low_back(product(attended, out_w.T))
    hidden = tokens + post_norm(branch, attn_g)
    mid_low = low(hidden)
    gate_pre = low_back(product(mid_low, gate_w))
    up_pre = low_back(product(mid_low, up_w))
    mixed = low(jax.nn.silu(gate_pre) * up_pre)
    ffn = low_back(product(mixed, down_w.T))
    return hidden + post_norm(ffn, ffn_g)

def reference(inputs, query_weight, key_weight, value_weight, out_weight, query_gain, key_gain, attn_gain, gate_weight, up_weight, down_weight, ffn_gain, positions, block_ids, cotangent):
    params = tuple((w.astype(jnp.float32) for w in (query_weight, key_weight, value_weight, out_weight, query_gain, key_gain, attn_gain, gate_weight, up_weight, down_weight, ffn_gain)))

    def one_sequence(totals, seq_data):
        tokens, position_ids, block_row, cot_seq = seq_data
        cosine, sine = rope_tables(position_ids)
        allowed = block_row[None, :] <= block_row[:, None]

        def apply(tok_f, *weights):
            return layer(tok_f, weights, cosine, sine, allowed)
        result, pullback = jax.vjp(apply, tokens.astype(jnp.float32), *params)
        grads = pullback(cot_seq.astype(jnp.float32))
        totals = tuple((acc + new for acc, new in zip(totals, grads[1:])))
        return (totals, (result.astype(jnp.bfloat16), grads[0]))
    zeros = tuple((jnp.zeros_like(w) for w in params))
    totals, (outputs, input_grads) = lax.scan(one_sequence, zeros, (inputs, positions, block_ids, cotangent))
    return (outputs, input_grads, totals[0], totals[1], totals[2], totals[3], totals[4], totals[5], totals[6], totals[7], totals[8], totals[9], totals[10])
```

```python
import jax
import jax.numpy as jnp
from jax import lax
from jax.sharding import PartitionSpec as P

D = 2048
HD = 128
EPS = 1e-06
THETA = 500000.0
NEG_FILL = -1e30
BF = jnp.bfloat16
F32 = jnp.float32


def dot(left, right):
    return jnp.dot(left, right, preferred_element_type=F32)


def dot_nt(left, right):
    return lax.dot_general(left, right, (((1,), (1,)), ((), ())), preferred_element_type=F32)


def dot_tn(left, right):
    return lax.dot_general(left, right, (((0,), (0,)), ((), ())), preferred_element_type=F32)


class Link:
    def __init__(self, axis, perm, depth):
        self.axis = axis
        self.perm = perm
        self.depth = depth
        self.done = []

    def send(self, array):
        if len(self.done) >= self.depth:
            array, _ = lax.optimization_barrier((array, self.done[-self.depth]))
        result = lax.ppermute(array, self.axis, self.perm)
        self.done.append(result)
        return result


def rope_tables(position_ids):
    inv_freq = 1.0 / THETA ** (jnp.arange(0, HD, 2, dtype=F32) / HD)
    angles = position_ids.astype(F32)[:, None] * inv_freq[None, :]
    angles = jnp.concatenate([angles, angles], axis=1)
    return (jnp.cos(angles), jnp.sin(angles))


def turn_heads(values, cosine, sine):
    half_width = values.shape[-1] // 2
    rotated = jnp.concatenate([-values[..., half_width:], values[..., :half_width]], axis=-1)
    return values * cosine[:, None, :] + rotated * sine[:, None, :]


def turn_back(grads, cosine, sine):
    half_width = grads.shape[-1] // 2
    scaled = grads * sine[:, None, :]
    moved_part = jnp.concatenate([scaled[..., half_width:], -scaled[..., :half_width]], axis=-1)
    return grads * cosine[:, None, :] + moved_part


def norm_back(source, inv_scale, gain_vec, grad_in):
    scaled = grad_in * gain_vec
    return inv_scale * scaled - source * inv_scale**3 * jnp.mean(
        source * scaled, axis=1, keepdims=True
    )


def body(
    inputs,
    query_weight,
    key_weight,
    value_weight,
    out_weight,
    query_gain,
    key_gain,
    attn_gain,
    gate_weight,
    up_weight,
    down_weight,
    ffn_gain,
    positions,
    block_ids,
    cotangent,
):
    dp = lax.axis_size("dp")
    ring = dp // 2
    width = D // dp
    pair = 2 * width
    seqs, rows, _ = inputs.shape
    local = seqs * rows
    tokens = 4 * local
    length = 4 * rows
    heads = query_weight.shape[1] // HD
    hw = heads * HD
    dp_index = lax.axis_index("dp")
    place, side = dp_index // 2, dp_index % 2
    t_index = lax.axis_index("tensor")
    t_high, t_low = t_index // 2, t_index % 2

    z_perm = [(i, (i - 2) % dp) for i in range(dp)]
    x_perm = [(i, i ^ 1) for i in range(dp)]
    y_perm = [(i, i ^ 2) for i in range(4)]
    c_perm = [(i, i ^ 1) for i in range(4)]

    def swap_sides(array):
        parts = array.reshape(array.shape[:-1] + (ring, 2, width))
        return jnp.where(side == 1, parts[..., ::-1, :], parts).reshape(array.shape)

    def roll(array, by):
        return lax.dynamic_slice_in_dim(
            jnp.concatenate([array, array], axis=-1), by, D, array.ndim - 1
        )

    def to_own(array):
        return swap_sides(roll(array, place * pair))

    def from_own(array):
        return roll(swap_sides(array), (D - place * pair) % D)

    def flip_rows(array, axis):
        parts = array.reshape(array.shape[:axis] + (2, 2) + array.shape[axis + 1 :])
        parts = jnp.where(t_high == 1, jnp.flip(parts, axis), parts)
        parts = jnp.where(t_low == 1, jnp.flip(parts, axis + 1), parts)
        return parts.reshape(array.shape)

    z_link = Link("dp", z_perm, 2)
    x_link = Link("dp", x_perm, 2)
    y_link = Link("tensor", y_perm, 2)

    def core_send(array):
        return lax.ppermute(array, "tensor", c_perm)

    def spread(own):
        other = core_send(own)
        far = y_link.send(own)
        return jnp.concatenate([own, other, far, core_send(far)], axis=0)

    def row_total(term, source):
        blocks = [source[u * local : (u + 1) * local] for u in range(4)]
        away = core_send(term(jnp.concatenate([blocks[1], blocks[3]], axis=0)))
        far = term(blocks[2]) + away[local:]
        back = y_link.send(far.astype(BF))
        return term(blocks[0]) + away[:local] + back.astype(F32)

    def sum_rows(vectors):
        parts = flip_rows(vectors.reshape(-1, 4, local), 1)
        return flip_rows(lax.psum(parts, "tensor"), 1).reshape(vectors.shape)

    def gather_steps(shard, pair_first):
        own, other = [shard] + [None] * (ring - 1), [None] * ring
        z_ops, x_ops = [], []

        def z_own(s):
            own[s] = z_link.send(own[s - 1])

        def z_other(s):
            other[s] = z_link.send(other[s - 1])

        def x_own(s):
            other[s] = x_link.send(own[s])

        return own, other, z_own, z_other, x_own

    qkv_shard = jnp.concatenate([query_weight, key_weight, value_weight], axis=1)
    streams = {}
    for name, shard in (
        ("qkv", qkv_shard),
        ("out", out_weight),
        ("gate", gate_weight),
        ("up", up_weight),
        ("down", down_weight),
    ):
        streams[name] = gather_steps(shard, name == "qkv")

    def run_z(name, s):
        streams[name][2](s)

    def run_zo(name, s):
        streams[name][3](s)

    def run_x(name, s):
        streams[name][4](s)

    x_own_rows = to_own(inputs.reshape(local, D))
    run_x("qkv", 0)
    tok_full = spread(x_own_rows)
    for s in range(1, ring):
        run_z("qkv", s)
        run_zo("qkv", s)
    for name in ("out", "gate", "up", "down"):
        run_x(name, 0)
    for name in ("out", "gate", "up", "down"):
        for s in range(1, ring):
            run_z(name, s)
            run_x(name, s)

    def stacked(name):
        own, other = streams[name][0], streams[name][1]
        blocks = []
        for s in range(ring):
            blocks += [own[s], other[s]]
        return jnp.concatenate(blocks, axis=0)

    attn_g, ffn_g = to_own(attn_gain[None]), to_own(ffn_gain[None])
    cot_rows = to_own(cotangent.reshape(local, D))

    qkv_w = stacked("qkv")
    pre = dot(tok_full, qkv_w)
    query_pre, key_pre = pre[:, :hw], pre[:, hw : 2 * hw]
    value_low = pre[:, 2 * hw :].astype(BF)
    squares = sum_rows(
        jnp.stack([jnp.sum(query_pre * query_pre, axis=1), jnp.sum(key_pre * key_pre, axis=1)])
    )
    inverses = lax.rsqrt(squares / D + EPS)
    query_inv, key_inv = inverses[0][:, None], inverses[1][:, None]
    own_positions = flip_rows(positions.reshape(seqs, 4, rows), 1)
    cosine, sine = rope_tables(own_positions.transpose(1, 0, 2).reshape(tokens))
    own_ids = flip_rows(block_ids.reshape(seqs, 4, rows), 1).reshape(seqs, length)
    allowed = own_ids[:, None, :] <= own_ids[:, :, None]

    def by_head(array):
        return (
            array.reshape(4, seqs, rows, heads, HD)
            .transpose(1, 3, 0, 2, 4)
            .reshape(seqs, heads, length, HD)
        )

    def by_token(array):
        return (
            array.reshape(seqs, heads, 4, rows, HD).transpose(2, 0, 3, 1, 4).reshape(tokens, hw)
        )

    query_rot = by_head(
        turn_heads(
            (query_pre * query_inv * query_gain).reshape(tokens, heads, HD), cosine, sine
        ).astype(BF)
    )
    key_rot = by_head(
        turn_heads(
            (key_pre * key_inv * key_gain).reshape(tokens, heads, HD), cosine, sine
        ).astype(BF)
    )
    value_heads = by_head(value_low)
    scores = (
        jnp.einsum("shqd,shkd->shqk", query_rot, key_rot, preferred_element_type=F32) * HD**-0.5
    )
    scores = jnp.where(allowed[:, None], scores, NEG_FILL)
    row_max = jnp.max(scores, axis=3, keepdims=True)
    exp_scores = jnp.exp(scores - row_max)
    probs = exp_scores / jnp.sum(exp_scores, axis=3, keepdims=True)
    probs_low = probs.astype(BF)
    attended = by_token(
        jnp.einsum("shqk,shkd->shqd", probs_low, value_heads, preferred_element_type=F32).astype(BF)
    )
    out_w = stacked("out")
    attn_rows = row_total(lambda part: dot_nt(part, out_w), attended)
    attn_inv = lax.rsqrt(jnp.mean(attn_rows * attn_rows, axis=1, keepdims=True) + EPS)
    hidden_rows = x_own_rows.astype(F32) + attn_rows * attn_inv * attn_g
    mid_full = spread(hidden_rows.astype(BF))
    gate_w, up_w = stacked("gate"), stacked("up")
    gate_pre = dot(mid_full, gate_w)
    up_pre = dot(mid_full, up_w)
    gate_sig = jax.nn.sigmoid(gate_pre)
    mixed = (gate_pre * gate_sig * up_pre).astype(BF)
    ffn_parts = []
    down_parts = []
    for s in range(ring):
        piece = jnp.concatenate([streams["down"][0][s], streams["down"][1][s]], axis=0)
        down_parts.append(piece)
        ffn_parts.append(row_total(lambda part, piece=piece: dot_nt(part, piece), mixed))
    down_w = jnp.concatenate(down_parts, axis=0)
    ffn_rows = jnp.concatenate(ffn_parts, axis=1)
    ffn_inv = lax.rsqrt(jnp.mean(ffn_rows * ffn_rows, axis=1, keepdims=True) + EPS)
    output_rows = hidden_rows + ffn_rows * ffn_inv * ffn_g

    def reduce_steps(chunk, pair_first):
        state = {}

        def x_first(s):
            state[("x", s)] = x_link.send(chunk(s, 1).astype(BF))

        def z_hop(s, t=0):
            state[("z", s - 1, t)] = z_link.send(total(s, t).astype(BF))

        def total(s, t):
            value = chunk(s, t)
            if pair_first:
                value = value + state[("x", s)].astype(F32)
            if s < ring - 1 and ("z", s, t) in state:
                value = value + state[("z", s, t)].astype(F32)
            return value

        return state, x_first, z_hop, total

    def reduce_stream(chunk, pair_first):
        received = {}

        def total(s, t):
            value = chunk(s, t)
            if pair_first:
                value = value + received[("x", s)].astype(F32)
            if (s, t) in received:
                value = value + received[(s, t)].astype(F32)
            return value

        def x_send(s):
            received[("x", s)] = x_link.send(chunk(s, 1).astype(BF))

        def z_send(s, t=0):
            received[((s + 1) % ring, t)] = z_link.send(total(s, t).astype(BF))

        def finish():
            if pair_first:
                return total(0, 0)
            back = x_link.send(total(0, 1).astype(BF))
            return total(0, 0) + back.astype(F32)

        return x_send, z_send, finish

    order = list(range(1, ring)) + [0]

    def run_reduce(stream, pair_first):
        x_send, z_send, finish = stream
        if pair_first:
            for s in order:
                x_send(s)
            for s in range(1, ring):
                z_send(s)
        else:
            for s in range(1, ring):
                z_send(s, 0)
                z_send(s, 1)
        return finish()

    def columns(full, s, t):
        return lax.slice_in_dim(full, s * pair + t * width, s * pair + (t + 1) * width, axis=1)

    ffn_back = norm_back(ffn_rows, ffn_inv, ffn_g, cot_rows)
    ffn_gain_part = jnp.sum(cot_rows * ffn_rows * ffn_inv, axis=0)
    ffn_back_low = ffn_back.astype(BF)
    back_parts = {}
    for s in order:
        back_parts[s] = spread(lax.slice_in_dim(ffn_back_low, s * pair, (s + 1) * pair, axis=1))
    ffn_back_full = jnp.concatenate([back_parts[s] for s in range(ring)], axis=1)

    down_grad = run_reduce(
        reduce_stream(
            lambda s, t: dot_tn(
                lax.slice_in_dim(back_parts[s], t * width, (t + 1) * width, axis=1), mixed
            ),
            True,
        ),
        True,
    )
    mixed_grad = dot(ffn_back_full, down_w)
    gate_low = (mixed_grad * up_pre * gate_sig * (1.0 + gate_pre * (1.0 - gate_sig))).astype(BF)
    up_low = (mixed_grad * gate_pre * gate_sig).astype(BF)
    gate_grad = run_reduce(
        reduce_stream(lambda s, t: dot_tn(columns(mid_full, s, t), gate_low), True), True
    )
    gate_up = jnp.concatenate([gate_low, up_low], axis=1)

    def mid_term(part):
        return dot_nt(part[:, : gate_low.shape[1]], gate_w) + dot_nt(
            part[:, gate_low.shape[1] :], up_w
        )

    hidden_grad = cot_rows + row_total(mid_term, gate_up)
    attn_back = norm_back(attn_rows, attn_inv, attn_g, hidden_grad)
    attn_gain_part = jnp.sum(hidden_grad * attn_rows * attn_inv, axis=0)
    attn_back_full = spread(attn_back.astype(BF))
    attended_grad = by_head(dot(attn_back_full, out_w).astype(BF))
    prob_grad = jnp.einsum(
        "shqd,shkd->shqk", attended_grad, value_heads, preferred_element_type=F32
    )
    inner_sum = jnp.sum(probs * prob_grad, axis=3, keepdims=True)
    score_low = (probs * (prob_grad - inner_sum)).astype(BF)
    query_rot_grad = by_token(
        jnp.einsum("shqk,shkd->shqd", score_low, key_rot, preferred_element_type=F32) * HD**-0.5
    )
    key_rot_grad = by_token(
        jnp.einsum("shqk,shqd->shkd", score_low, query_rot, preferred_element_type=F32) * HD**-0.5
    )
    value_back = by_token(
        jnp.einsum(
            "shqk,shqd->shkd", probs_low, attended_grad, preferred_element_type=F32
        ).astype(BF)
    )
    query_norm_grad = turn_back(query_rot_grad.reshape(tokens, heads, HD), cosine, sine).reshape(
        tokens, hw
    )
    key_norm_grad = turn_back(key_rot_grad.reshape(tokens, heads, HD), cosine, sine).reshape(
        tokens, hw
    )
    query_gain_part = jnp.sum(query_norm_grad * query_pre * query_inv, axis=0)
    key_gain_part = jnp.sum(key_norm_grad * key_pre * key_inv, axis=0)
    query_scaled = query_norm_grad * query_gain
    key_scaled = key_norm_grad * key_gain
    dots = sum_rows(
        jnp.stack([jnp.sum(query_pre * query_scaled, axis=1), jnp.sum(key_pre * key_scaled, axis=1)])
    )
    query_dot, key_dot = dots[0][:, None], dots[1][:, None]
    query_low = (
        query_inv * query_scaled - query_pre * query_inv**3 * (query_dot / D)
    ).astype(BF)
    key_low = (key_inv * key_scaled - key_pre * key_inv**3 * (key_dot / D)).astype(BF)
    qkv_low = jnp.concatenate([query_low, key_low, value_back], axis=1)
    input_rows = hidden_grad + row_total(lambda part: dot_nt(part, qkv_w), qkv_low)

    up_grad = run_reduce(
        reduce_stream(lambda s, t: dot_tn(columns(mid_full, s, t), up_low), True), True
    )
    qkv_grad = run_reduce(
        reduce_stream(lambda s, t: dot_tn(columns(tok_full, s, t), qkv_low), False), False
    )
    out_grad = run_reduce(
        reduce_stream(lambda s, t: dot_tn(columns(attn_back_full, s, t), attended), True), True
    )

    offset = t_index * hw
    query_full = lax.dynamic_update_slice(jnp.zeros((D,), F32), query_gain_part, (offset,))
    key_full = lax.dynamic_update_slice(jnp.zeros((D,), F32), key_gain_part, (offset,))
    query_total, key_total, attn_total, ffn_total = lax.psum(
        (query_full, key_full, from_own(attn_gain_part[None])[0], from_own(ffn_gain_part[None])[0]),
        ("dp", "tensor"),
    )
    return (
        from_own(output_rows.astype(BF)).reshape(inputs.shape),
        from_own(input_rows).reshape(inputs.shape),
        qkv_grad[:, :hw],
        qkv_grad[:, hw : 2 * hw],
        qkv_grad[:, 2 * hw :],
        out_grad,
        lax.dynamic_slice(query_total, (offset,), (hw,)),
        lax.dynamic_slice(key_total, (offset,), (hw,)),
        attn_total,
        gate_grad,
        up_grad,
        down_grad,
        ffn_total,
    )


def solution(mesh):
    whole = P()
    both = P("dp", "tensor")
    rows = P("dp", "tensor", None)
    lanes = P("tensor")
    return jax.shard_map(
        body,
        mesh=mesh,
        in_specs=(
            rows, both, both, both, both, lanes, lanes, whole, both, both, both, whole,
            P("dp", None), P("dp", None), rows,
        ),
        out_specs=(
            rows, rows, both, both, both, both, lanes, lanes, whole, both, both, both, whole,
        ),
        check_vma=False,
    )
```

```python
import jax
import jax.numpy as jnp
from jax import lax
from jax.sharding import PartitionSpec as P

D = 2048
HD = 128
EPS = 1e-06
THETA = 500000.0
NEG_FILL = -1e30
BF = jnp.bfloat16
F32 = jnp.float32


def dot(left, right):
    return jnp.dot(left, right, preferred_element_type=F32)


def dot_nt(left, right):
    return lax.dot_general(left, right, (((1,), (1,)), ((), ())), preferred_element_type=F32)


def dot_tn(left, right):
    return lax.dot_general(left, right, (((0,), (0,)), ((), ())), preferred_element_type=F32)


def after(array, others):
    return lax.optimization_barrier((array, others))[0]


def rope_tables(position_ids):
    inv_freq = 1.0 / THETA ** (jnp.arange(0, HD, 2, dtype=F32) / HD)
    angles = position_ids.astype(F32)[:, None] * inv_freq[None, :]
    angles = jnp.concatenate([angles, angles], axis=1)
    return (jnp.cos(angles), jnp.sin(angles))


def turn_heads(values, cosine, sine):
    half_width = values.shape[-1] // 2
    rotated = jnp.concatenate([-values[..., half_width:], values[..., :half_width]], axis=-1)
    return values * cosine[:, None, :] + rotated * sine[:, None, :]


def turn_back(grads, cosine, sine):
    half_width = grads.shape[-1] // 2
    scaled = grads * sine[:, None, :]
    moved_part = jnp.concatenate([scaled[..., half_width:], -scaled[..., :half_width]], axis=-1)
    return grads * cosine[:, None, :] + moved_part


def norm_back(source, inv_scale, gain_vec, grad_in):
    scaled = grad_in * gain_vec
    return inv_scale * scaled - source * inv_scale**3 * jnp.mean(
        source * scaled, axis=1, keepdims=True
    )


def body(
    inputs,
    query_weight,
    key_weight,
    value_weight,
    out_weight,
    query_gain,
    key_gain,
    attn_gain,
    gate_weight,
    up_weight,
    down_weight,
    ffn_gain,
    positions,
    block_ids,
    cotangent,
):
    dp = lax.axis_size("dp")
    seqs, rows, _ = inputs.shape
    local = seqs * rows
    tokens = 8 * local
    length = 4 * rows
    hw = query_weight.shape[1] // 2
    heads = hw // HD
    half = D // 2
    side = lax.axis_index("dp") % 2
    t_index = lax.axis_index("tensor")
    t_high, t_low = t_index // 2, t_index % 2

    x_perm = [(i, i ^ 1) for i in range(dp)]
    y_perm = [(i, i ^ 2) for i in range(4)]
    c_perm = [(i, i ^ 1) for i in range(4)]
    z_groups = [list(range(0, dp, 2)), list(range(1, dp, 2))]

    def x_send(array):
        return lax.ppermute(array, "dp", x_perm)

    def y_send(array):
        return lax.ppermute(array, "tensor", y_perm)

    def core_send(array):
        return lax.ppermute(array, "tensor", c_perm)

    def by_side(mine, other, axis):
        return jnp.concatenate(
            [jnp.where(side == 0, mine, other), jnp.where(side == 0, other, mine)], axis=axis
        )

    def column_half(array, which):
        width = array.shape[-1] // 2
        return lax.dynamic_slice_in_dim(array, which * width, width, array.ndim - 1)

    def pair_rows(*weights):
        mine = jnp.concatenate([column_half(w, side) for w in weights], axis=1)
        theirs = jnp.concatenate([column_half(w, 1 - side) for w in weights], axis=1)
        return mine, x_send(theirs)

    def gather(*weights):
        mine, other = pair_rows(*weights)
        return lax.all_gather(
            by_side(mine, other, 0), "dp", axis=0, tiled=True, axis_index_groups=z_groups
        )

    def reduce_grad(features, grads):
        summed = lax.psum_scatter(
            dot_tn(features, grads).astype(BF),
            "dp",
            scatter_dimension=0,
            tiled=True,
            axis_index_groups=z_groups,
        )
        width = summed.shape[0] // 2
        mine = lax.dynamic_slice_in_dim(summed, side * width, width, 0)
        theirs = lax.dynamic_slice_in_dim(summed, (1 - side) * width, width, 0)
        return mine, x_send(theirs)

    def flip_rows(array, axis):
        parts = array.reshape(array.shape[:axis] + (2, 2) + array.shape[axis + 1 :])
        parts = jnp.where(t_high == 1, jnp.flip(parts, axis), parts)
        parts = jnp.where(t_low == 1, jnp.flip(parts, axis + 1), parts)
        return parts.reshape(array.shape)

    def spread(own):
        first, second = own[:, :half], own[:, half:]
        x_first, y_second = x_send(first), y_send(second)
        first_pair = jnp.concatenate([first, x_first], axis=0)
        second_pair = jnp.concatenate([second, y_second], axis=0)
        y_first, x_second = y_send(first_pair), x_send(second_pair)
        low = jnp.concatenate(
            [first, y_first[:local], x_first, y_first[local:]], axis=0
        )
        high = jnp.concatenate([second_pair, x_second], axis=0)
        even = jnp.concatenate([low, high], axis=1)
        odd = core_send(even)
        blocks = []
        for a in range(2):
            for u in range(2):
                at = (2 * a + u) * local
                blocks += [even[at : at + local], odd[at : at + local]]
        return jnp.concatenate(blocks, axis=0)

    def row_total(term, source):
        blocks = [source[i * local : (i + 1) * local] for i in range(8)]
        away = core_send(term(jnp.concatenate(blocks[1::2], axis=0)).astype(BF))
        kept = term(jnp.concatenate(blocks[0::2], axis=0)) + away.astype(F32)
        low, high = kept[:, :half], kept[:, half:]
        x_low = x_send(low[2 * local :].astype(BF))
        y_high = y_send(
            jnp.concatenate([high[local : 2 * local], high[3 * local :]], axis=0).astype(BF)
        )
        low = low[: 2 * local] + x_low.astype(F32)
        high_own = high[:local] + y_high[:local].astype(F32)
        high_other = high[2 * local : 3 * local] + y_high[local:].astype(F32)
        y_low = y_send(low[local:].astype(BF))
        x_high = x_send(high_other.astype(BF))
        return jnp.concatenate(
            [low[:local] + y_low.astype(F32), high_own + x_high.astype(F32)], axis=1
        )

    def sum_rows(vectors):
        parts = flip_rows(vectors.reshape(-1, 2, 4, local), 2)
        parts = lax.psum(parts, "tensor")
        parts = parts + x_send(parts[:, ::-1])
        return flip_rows(parts, 2).reshape(vectors.shape)

    qkv_w = gather(query_weight, key_weight, value_weight)
    out_w = gather(out_weight)
    gate_w = gather(gate_weight)
    up_w = gather(up_weight)
    down_w = gather(down_weight)
    own_tokens = inputs.reshape(local, D)
    tok_full = spread(own_tokens)
    attn_g, ffn_g = attn_gain[None], ffn_gain[None]
    query_g, key_g = column_half(query_gain, side), column_half(key_gain, side)
    cot_rows = cotangent.reshape(local, D)

    pre = dot(tok_full, qkv_w)
    query_pre, key_pre = pre[:, :hw], pre[:, hw : 2 * hw]
    value_low = pre[:, 2 * hw :].astype(BF)
    squares = sum_rows(
        jnp.stack([jnp.sum(query_pre * query_pre, axis=1), jnp.sum(key_pre * key_pre, axis=1)])
    )
    inverses = lax.rsqrt(squares / D + EPS)
    query_inv, key_inv = inverses[0][:, None], inverses[1][:, None]
    marks = jnp.stack([positions, block_ids])
    marks = jnp.stack([marks, x_send(marks)], axis=1)
    marks = flip_rows(marks.reshape(2, 2, seqs, 4, rows), 3)
    cosine, sine = rope_tables(marks[0].transpose(0, 2, 1, 3).reshape(tokens))
    own_ids = marks[1].reshape(2 * seqs, length)
    allowed = own_ids[:, None, :] <= own_ids[:, :, None]

    def by_head(array):
        return (
            array.reshape(2, 4, seqs, rows, heads, HD)
            .transpose(0, 2, 4, 1, 3, 5)
            .reshape(2 * seqs, heads, length, HD)
        )

    def by_token(array):
        return (
            array.reshape(2, seqs, heads, 4, rows, HD)
            .transpose(0, 3, 1, 4, 2, 5)
            .reshape(tokens, hw)
        )

    query_rot = by_head(
        turn_heads(
            (query_pre * query_inv * query_g).reshape(tokens, heads, HD), cosine, sine
        ).astype(BF)
    )
    key_rot = by_head(
        turn_heads((key_pre * key_inv * key_g).reshape(tokens, heads, HD), cosine, sine).astype(BF)
    )
    value_heads = by_head(value_low)
    scores = (
        jnp.einsum("shqd,shkd->shqk", query_rot, key_rot, preferred_element_type=F32) * HD**-0.5
    )
    scores = jnp.where(allowed[:, None], scores, NEG_FILL)
    row_max = jnp.max(scores, axis=3, keepdims=True)
    exp_scores = jnp.exp(scores - row_max)
    probs = exp_scores / jnp.sum(exp_scores, axis=3, keepdims=True)
    probs_low = probs.astype(BF)
    attended = by_token(
        jnp.einsum("shqk,shkd->shqd", probs_low, value_heads, preferred_element_type=F32).astype(BF)
    )
    attn_rows = row_total(lambda part: dot_nt(part, out_w), attended)
    attn_inv = lax.rsqrt(jnp.mean(attn_rows * attn_rows, axis=1, keepdims=True) + EPS)
    hidden_rows = own_tokens.astype(F32) + attn_rows * attn_inv * attn_g
    mid_full = spread(hidden_rows.astype(BF))
    gate_pre = dot(mid_full, gate_w)
    up_pre = dot(mid_full, up_w)
    gate_sig = jax.nn.sigmoid(gate_pre)
    mixed = (gate_pre * gate_sig * up_pre).astype(BF)
    ffn_rows = row_total(lambda part: dot_nt(part, down_w), mixed)
    ffn_inv = lax.rsqrt(jnp.mean(ffn_rows * ffn_rows, axis=1, keepdims=True) + EPS)
    output_rows = hidden_rows + ffn_rows * ffn_inv * ffn_g

    ffn_back = norm_back(ffn_rows, ffn_inv, ffn_g, cot_rows)
    ffn_gain_part = jnp.sum(cot_rows * ffn_rows * ffn_inv, axis=0)
    ffn_back_full = spread(ffn_back.astype(BF))
    down_grad = reduce_grad(ffn_back_full, mixed)
    mixed_grad = dot(ffn_back_full, down_w)
    gate_low = (mixed_grad * up_pre * gate_sig * (1.0 + gate_pre * (1.0 - gate_sig))).astype(BF)
    up_low = (mixed_grad * gate_pre * gate_sig).astype(BF)
    gate_grad = reduce_grad(mid_full, gate_low)
    up_grad = reduce_grad(mid_full, up_low)
    units = gate_low.shape[1]

    def mid_term(part):
        return dot_nt(part[:, :units], gate_w) + dot_nt(part[:, units:], up_w)

    hidden_grad = cot_rows + row_total(mid_term, jnp.concatenate([gate_low, up_low], axis=1))
    attn_back = norm_back(attn_rows, attn_inv, attn_g, hidden_grad)
    attn_gain_part = jnp.sum(hidden_grad * attn_rows * attn_inv, axis=0)
    attn_back_full = spread(attn_back.astype(BF))
    out_grad = reduce_grad(attn_back_full, attended)
    attended_grad = by_head(dot(attn_back_full, out_w).astype(BF))
    prob_grad = jnp.einsum(
        "shqd,shkd->shqk", attended_grad, value_heads, preferred_element_type=F32
    )
    inner_sum = jnp.sum(probs * prob_grad, axis=3, keepdims=True)
    score_low = (probs * (prob_grad - inner_sum)).astype(BF)
    query_rot_grad = by_token(
        jnp.einsum("shqk,shkd->shqd", score_low, key_rot, preferred_element_type=F32) * HD**-0.5
    )
    key_rot_grad = by_token(
        jnp.einsum("shqk,shqd->shkd", score_low, query_rot, preferred_element_type=F32) * HD**-0.5
    )
    value_back = by_token(
        jnp.einsum(
            "shqk,shqd->shkd", probs_low, attended_grad, preferred_element_type=F32
        ).astype(BF)
    )
    query_norm_grad = turn_back(query_rot_grad.reshape(tokens, heads, HD), cosine, sine).reshape(
        tokens, hw
    )
    key_norm_grad = turn_back(key_rot_grad.reshape(tokens, heads, HD), cosine, sine).reshape(
        tokens, hw
    )
    query_gain_part = jnp.sum(query_norm_grad * query_pre * query_inv, axis=0)
    key_gain_part = jnp.sum(key_norm_grad * key_pre * key_inv, axis=0)
    query_scaled = query_norm_grad * query_g
    key_scaled = key_norm_grad * key_g
    dots = sum_rows(
        jnp.stack([jnp.sum(query_pre * query_scaled, axis=1), jnp.sum(key_pre * key_scaled, axis=1)])
    )
    query_dot, key_dot = dots[0][:, None], dots[1][:, None]
    query_low = (query_inv * query_scaled - query_pre * query_inv**3 * (query_dot / D)).astype(BF)
    key_low = (key_inv * key_scaled - key_pre * key_inv**3 * (key_dot / D)).astype(BF)
    qkv_low = jnp.concatenate([query_low, key_low, value_back], axis=1)
    qkv_grad = reduce_grad(tok_full, qkv_low)
    input_rows = hidden_grad + row_total(lambda part: dot_nt(part, qkv_w), qkv_low)

    def own_columns(grad):
        return by_side(grad[0], grad[1], 1).astype(F32)

    def own_thirds(grad, which):
        return own_columns([part[:, which * hw : (which + 1) * hw] for part in grad])

    def sum_dp(array):
        step = 1
        while step < dp:
            array = array + lax.ppermute(array, "dp", [(i, i ^ step) for i in range(dp)])
            step *= 2
        return array

    def placed(part):
        return lax.dynamic_update_slice(jnp.zeros((2 * hw,), F32), part, (side * hw,))

    shared = jnp.stack([attn_gain_part, ffn_gain_part])
    shared = shared + core_send(shared)
    shared = shared + y_send(shared)
    gains = sum_dp(
        jnp.concatenate(
            [placed(query_gain_part), placed(key_gain_part), shared.reshape(-1)]
        ).reshape(-1, HD)
    ).reshape(-1)
    return (
        output_rows.astype(BF).reshape(inputs.shape),
        input_rows.reshape(inputs.shape),
        own_thirds(qkv_grad, 0),
        own_thirds(qkv_grad, 1),
        own_thirds(qkv_grad, 2),
        own_columns(out_grad),
        gains[: 2 * hw],
        gains[2 * hw : 4 * hw],
        gains[4 * hw : 4 * hw + D],
        own_columns(gate_grad),
        own_columns(up_grad),
        own_columns(down_grad),
        gains[4 * hw + D :],
    )


def solution(mesh):
    whole = P()
    both = P("dp", "tensor")
    rows = P("dp", "tensor", None)
    lanes = P("tensor")
    return jax.shard_map(
        body,
        mesh=mesh,
        in_specs=(
            rows, both, both, both, both, lanes, lanes, whole, both, both, both, whole,
            P("dp", None), P("dp", None), rows,
        ),
        out_specs=(
            rows, rows, both, both, both, both, lanes, lanes, whole, both, both, both, whole,
        ),
        check_vma=False,
    )
```

```python
import jax
import jax.numpy as jnp
from jax import lax
from jax.experimental import pallas as pl
from jax.experimental.pallas import tpu as pltpu
from jax.sharding import PartitionSpec as P

D = 2048
HD = 128
EPS = 1e-06
THETA = 500000.0
NEG_FILL = -1e30
BF = jnp.bfloat16
F32 = jnp.float32


def dot(left, right):
    return jnp.dot(left, right, preferred_element_type=F32)


def dot_nt(left, right):
    return lax.dot_general(left, right, (((1,), (1,)), ((), ())), preferred_element_type=F32)


def dot_tn(left, right):
    return lax.dot_general(left, right, (((0,), (0,)), ((), ())), preferred_element_type=F32)


def after(array, others):
    return lax.optimization_barrier((array, others))[0]


def rope_tables(position_ids):
    inv_freq = 1.0 / THETA ** (jnp.arange(0, HD, 2, dtype=F32) / HD)
    angles = position_ids.astype(F32)[:, None] * inv_freq[None, :]
    angles = jnp.concatenate([angles, angles], axis=1)
    return (jnp.cos(angles), jnp.sin(angles))


MESH = pl.DeviceIdType.MESH
SCALE = HD**-0.5


def place():
    d, t = lax.axis_index("dp"), lax.axis_index("tensor")
    side, high, low = d % 2, t // 2, t % 2
    partners = ({"dp": d + 1 - 2 * side}, {"tensor": t + 2 - 4 * high}, {"tensor": t + 1 - 2 * low})
    return side, high, low, t, partners


def greet(partners):
    barrier = pltpu.get_barrier_semaphore()
    for partner in partners:
        pl.semaphore_signal(barrier, inc=1, device_id=partner, device_id_type=MESH)
    pl.semaphore_wait(barrier, len(partners))


def remote(src, dst, send_sem, recv_sem, slot, partner):
    return pltpu.make_async_remote_copy(
        src_ref=src,
        dst_ref=dst,
        send_sem=send_sem.at[slot],
        recv_sem=recv_sem.at[slot],
        device_id=partner,
        device_id_type=MESH,
    )


def spread_kernel(own, out, own_sem, send_sem, recv_sem):
    side, high, low, t, partners = place()
    x_peer, y_peer, c_peer = partners
    t_y, other = t + 2 - 4 * high, 1 - side
    width = own.shape[2] // 4

    def part(a, b, i):
        return out.at[a, :, b, :, pl.ds(i * width, width)]

    greet(partners)

    def send(src, dst, slot, peer):
        copy = remote(src, dst, send_sem, recv_sem, slot, peer)
        copy.start()
        return copy

    def own_part(i):
        return own.at[:, :, pl.ds(i * width, width)]

    x_own, y_own = {}, {}
    for i, j in ((0, 2), (1, 3), (2, 0), (3, 1)):
        x_own[i] = send(own_part(i), part(side, t, i), i, x_peer)
        y_own[j] = send(own_part(j), part(side, t, j), 4 + j, y_peer)
    copies = list(x_own.values()) + list(y_own.values())
    core = [send(own, out.at[side, :, t], 12, c_peer)]
    local = pltpu.make_async_copy(own, out.at[side, :, t], own_sem)
    local.start()
    far = {}

    def to_core(a, b, i, slot):
        core.append(send(part(a, b, i), part(a, b, i), slot, c_peer))

    for i, j in ((0, 2), (1, 3)):
        x_own[i].wait_recv()
        far[i] = send(part(other, t, i), part(other, t, i), 8 + i, y_peer)
        to_core(other, t, i, 13 + i)
        y_own[j].wait_recv()
        far[j] = send(part(side, t_y, j), part(side, t_y, j), 8 + j, x_peer)
        to_core(side, t_y, j, 17 + j)
    for i, j in ((2, 0), (3, 1)):
        x_own[i].wait_recv()
        to_core(other, t, i, 13 + i)
        y_own[j].wait_recv()
        to_core(side, t_y, j, 17 + j)
    for i in (0, 2, 1, 3):
        far[i].wait_recv()
        to_core(other, t_y, i, 21 + i)
    for copy in core:
        copy.wait_recv()
    local.wait()
    for copy in copies + list(far.values()) + core:
        copy.wait_send()


def total_kernel(
    part, out, keep, from_core, x_in, y_in, x_last, y_last, local_sem, send_sem, recv_sem
):
    side, high, low, t, partners = place()
    x_peer, y_peer, c_peer = partners
    seqs, rows, width = out.shape
    half = width // 2
    first, second = pl.ds(0, half), pl.ds(half, half)
    greet(partners)

    def send(src, dst, slot, peer):
        copy = remote(src, dst, send_sem, recv_sem, slot, peer)
        copy.start()
        return copy

    core, local = {}, {}
    order = ((1, 1), (1, 0), (0, 1), (0, 0))
    for n, (ra, ry) in enumerate(order):
        a, b = (side + ra) % 2, 2 * ((high + ry) % 2)
        for s in range(seqs):
            core[ra, ry, s] = send(
                part.at[a, s, b + 1 - low], from_core.at[ra, ry, s], n * seqs + s, c_peer
            )
            local[ra, ry, s] = pltpu.make_async_copy(
                part.at[a, s, b + low], keep.at[ra, ry, s], local_sem.at[n * seqs + s]
            )
            local[ra, ry, s].start()

    def each(body):
        @pl.loop(0, rows // 16)
        def _(i):
            body(pl.ds(i * 16, 16))

    def add_core(ra, ry, s):
        local[ra, ry, s].wait()
        core[ra, ry, s].wait_recv()

        def step(at):
            total = keep[ra, ry, s, at].astype(F32) + from_core[ra, ry, s, at].astype(F32)
            if ra or ry:
                keep[ra, ry, s, at] = total.astype(BF)
            else:
                out[s, at] = total

        each(step)

    base = 4 * seqs
    x_far, y_far, x_near, y_near, x_end, y_end = {}, {}, {}, {}, {}, {}
    for s in range(seqs):
        add_core(1, 1, s)
        x_far[s] = send(keep.at[1, 1, s, :, first], x_in.at[0, s], base + s, x_peer)
        y_far[s] = send(keep.at[1, 1, s, :, second], y_in.at[0, s], base + seqs + s, y_peer)
    for s in range(seqs):
        add_core(1, 0, s)
        x_near[s] = send(keep.at[1, 0, s, :, first], x_in.at[1, s], base + 2 * seqs + s, x_peer)
        add_core(0, 1, s)
        y_near[s] = send(keep.at[0, 1, s, :, second], y_in.at[1, s], base + 3 * seqs + s, y_peer)
    for s in range(seqs):
        add_core(0, 0, s)
    for s in range(seqs):
        x_far[s].wait_recv()

        def step_x(at):
            keep[0, 1, s, at, first] = (
                keep[0, 1, s, at, first].astype(F32) + x_in[0, s, at].astype(F32)
            ).astype(BF)

        each(step_x)
        y_end[s] = send(keep.at[0, 1, s, :, first], y_last.at[s], base + 4 * seqs + s, y_peer)
        y_far[s].wait_recv()

        def step_y(at):
            keep[1, 0, s, at, second] = (
                keep[1, 0, s, at, second].astype(F32) + y_in[0, s, at].astype(F32)
            ).astype(BF)

        each(step_y)
        x_end[s] = send(keep.at[1, 0, s, :, second], x_last.at[s], base + 5 * seqs + s, x_peer)
    for s in range(seqs):
        x_near[s].wait_recv()
        y_near[s].wait_recv()

        def step_near(at):
            out[s, at, first] = out[s, at, first] + x_in[1, s, at].astype(F32)
            out[s, at, second] = out[s, at, second] + y_in[1, s, at].astype(F32)

        each(step_near)
    for s in range(seqs):
        x_end[s].wait_recv()
        y_end[s].wait_recv()

        def step_end(at):
            out[s, at, first] = out[s, at, first] + y_last[s, at].astype(F32)
            out[s, at, second] = out[s, at, second] + x_last[s, at].astype(F32)

        each(step_end)
    for group in (core, x_far, y_far, x_near, y_near, x_end, y_end):
        for copy in group.values():
            copy.wait_send()


def spread(own):
    seqs, rows, width = own.shape
    out = pl.pallas_call(
        spread_kernel,
        out_shape=jax.ShapeDtypeStruct((2, seqs, 4, rows, width), own.dtype),
        in_specs=[pl.BlockSpec(memory_space=pl.ANY)],
        out_specs=pl.BlockSpec(memory_space=pl.ANY),
        scratch_shapes=[
            pltpu.SemaphoreType.DMA,
            pltpu.SemaphoreType.DMA((25,)),
            pltpu.SemaphoreType.DMA((25,)),
        ],
        compiler_params=pltpu.CompilerParams(collective_id=0, has_side_effects=True),
        name="spread",
    )(own)
    return out.reshape(8 * seqs * rows, width)


def row_total(part, seqs):
    tokens, width = part.shape
    rows = tokens // (8 * seqs)
    half = width // 2
    out = pl.pallas_call(
        total_kernel,
        out_shape=jax.ShapeDtypeStruct((seqs, rows, width), F32),
        in_specs=[pl.BlockSpec(memory_space=pl.ANY)],
        out_specs=pl.BlockSpec(memory_space=pltpu.VMEM),
        scratch_shapes=[
            pltpu.VMEM((2, 2, seqs, rows, width), BF),
            pltpu.VMEM((2, 2, seqs, rows, width), BF),
            pltpu.VMEM((2, seqs, rows, half), BF),
            pltpu.VMEM((2, seqs, rows, half), BF),
            pltpu.VMEM((seqs, rows, half), BF),
            pltpu.VMEM((seqs, rows, half), BF),
            pltpu.SemaphoreType.DMA((4 * seqs,)),
            pltpu.SemaphoreType.DMA((10 * seqs,)),
            pltpu.SemaphoreType.DMA((10 * seqs,)),
        ],
        compiler_params=pltpu.CompilerParams(
            collective_id=1, has_side_effects=True, vmem_limit_bytes=32 << 20
        ),
        name="row_total",
    )(part.reshape(2, seqs, 4, rows, width))
    return out.reshape(seqs * rows, width)


def lane_sign(shape):
    return jnp.where(lax.broadcasted_iota(jnp.int32, shape, 1) < HD // 2, -1.0, 1.0)


def score_block(query, key, query_ids, key_ids):
    scores = dot_nt(query, key) * SCALE
    return jnp.where(key_ids > query_ids, NEG_FILL, scores)


def attend_kernel(
    q, k, v, inv, q_gain, k_gain, cosine, sine, column_ids, row_ids, q_out, k_out, att_out, log_out
):
    turn = sine[...] * lane_sign(sine.shape)

    def rotated(pre, column, gain):
        normed = pre[...] * inv[:, column : column + 1] * gain[...]
        return (normed * cosine[...] + pltpu.roll(normed, HD // 2, 1) * turn).astype(BF)

    query, key = rotated(q, 0, q_gain), rotated(k, 1, k_gain)
    scores = score_block(query, key, column_ids[...], row_ids[0])
    top = jnp.max(scores, axis=1, keepdims=True)
    grown = jnp.exp(scores - top)
    total = jnp.sum(grown, axis=1, keepdims=True)
    probs = (grown / total).astype(BF)
    att_out[...] = dot(probs, v[...].astype(BF)).astype(BF)
    q_out[...] = query
    k_out[...] = key
    log_out[0] = top + jnp.log(total)


def attend_back_kernel(
    q, k, v, inv, q_gain, k_gain, cosine, sine, column_ids, row_ids, query, key, grad, log_total,
    q_scaled, k_scaled, v_out, q_dot, k_dot, q_part, k_part,
):
    back = -lane_sign(sine.shape)
    scores = score_block(query[...], key[...], column_ids[...], row_ids[0])
    probs = jnp.exp(scores - log_total[0])
    prob_grad = dot_nt(grad[...], v[...].astype(BF))
    inner = jnp.sum(probs * prob_grad, axis=1, keepdims=True)
    score_grad = (probs * (prob_grad - inner)).astype(BF)
    v_out[...] = dot_tn(probs.astype(BF), grad[...]).astype(BF)

    def finish(rot_grad, pre, column, gain, scaled, dots, parts):
        normed = rot_grad * cosine[...] + pltpu.roll(rot_grad * sine[...], HD // 2, 1) * back
        parts[0] = jnp.sum(normed * pre[...] * inv[:, column : column + 1], axis=0, keepdims=True)
        normed = normed * gain[...]
        scaled[...] = normed
        dots[0] = jnp.sum(normed * pre[...], axis=1, keepdims=True)

    finish(dot(score_grad, key[...]) * SCALE, q, 0, q_gain, q_scaled, q_dot, q_part)
    finish(dot_tn(score_grad, query[...]) * SCALE, k, 1, k_gain, k_scaled, k_dot, k_part)


def attention_specs(length, heads):
    def tile(first):
        return pl.BlockSpec((length, HD), lambda s, h, first=first: (s, first + h))

    table = pl.BlockSpec((length, HD), lambda s, h: (s, 0))
    gain = pl.BlockSpec((1, HD), lambda s, h: (0, h))
    token = pl.BlockSpec((1, length, 1), lambda s, h: (h, s, 0))
    common = [
        tile(0),
        tile(heads),
        tile(2 * heads),
        pl.BlockSpec((length, 2), lambda s, h: (s, 0)),
        gain,
        gain,
        table,
        table,
        pl.BlockSpec((length, 1), lambda s, h: (s, 0)),
        pl.BlockSpec((1, 1, length), lambda s, h: (s, 0, 0)),
    ]
    return tile(0), token, common


def norm_back(source, inv_scale, gain_vec, grad_in):
    scaled = grad_in * gain_vec
    return inv_scale * scaled - source * inv_scale**3 * jnp.mean(
        source * scaled, axis=1, keepdims=True
    )


def body(
    inputs,
    query_weight,
    key_weight,
    value_weight,
    out_weight,
    query_gain,
    key_gain,
    attn_gain,
    gate_weight,
    up_weight,
    down_weight,
    ffn_gain,
    positions,
    block_ids,
    cotangent,
):
    dp = lax.axis_size("dp")
    seqs, rows, _ = inputs.shape
    local = seqs * rows
    tokens = 8 * local
    length = 4 * rows
    hw = query_weight.shape[1] // 2
    heads = hw // HD
    side = lax.axis_index("dp") % 2

    x_perm = [(i, i ^ 1) for i in range(dp)]
    y_perm = [(i, i ^ 2) for i in range(4)]
    c_perm = [(i, i ^ 1) for i in range(4)]
    z_groups = [list(range(0, dp, 2)), list(range(1, dp, 2))]

    def x_send(array):
        return lax.ppermute(array, "dp", x_perm)

    def y_send(array):
        return lax.ppermute(array, "tensor", y_perm)

    def core_send(array):
        return lax.ppermute(array, "tensor", c_perm)

    def by_side(mine, other, axis):
        return jnp.concatenate(
            [jnp.where(side == 0, mine, other), jnp.where(side == 0, other, mine)], axis=axis
        )

    def column_half(array, which):
        width = array.shape[-1] // 2
        return lax.dynamic_slice_in_dim(array, which * width, width, array.ndim - 1)

    def pair_rows(*weights):
        mine = jnp.concatenate([column_half(w, side) for w in weights], axis=1)
        theirs = jnp.concatenate([column_half(w, 1 - side) for w in weights], axis=1)
        return mine, x_send(theirs)

    def gather(*weights):
        mine, other = pair_rows(*weights)
        return lax.all_gather(
            by_side(mine, other, 0), "dp", axis=0, tiled=True, axis_index_groups=z_groups
        )

    def reduce_grad(features, grads):
        summed = lax.psum_scatter(
            dot_tn(features, grads).astype(BF),
            "dp",
            scatter_dimension=0,
            tiled=True,
            axis_index_groups=z_groups,
        )
        width = summed.shape[0] // 2
        mine = lax.dynamic_slice_in_dim(summed, side * width, width, 0)
        theirs = lax.dynamic_slice_in_dim(summed, (1 - side) * width, width, 0)
        return mine, x_send(theirs)

    def sum_rows(vectors):
        parts = lax.psum(vectors.reshape(-1, HD), "tensor")
        return (parts + x_send(parts)).reshape(vectors.shape)

    qkv_w = gather(query_weight, key_weight, value_weight)
    out_w = gather(out_weight)
    gate_w = gather(gate_weight)
    up_w = gather(up_weight)
    down_w = gather(down_weight)
    own_tokens = inputs.reshape(local, D)
    tok_full = spread(inputs)
    attn_g, ffn_g = attn_gain[None], ffn_gain[None]
    query_g, key_g = column_half(query_gain[None], side), column_half(key_gain[None], side)
    cot_rows = cotangent.reshape(local, D)

    pre = dot(tok_full, qkv_w)
    query_pre, key_pre = pre[:, :hw], pre[:, hw : 2 * hw]
    squares = sum_rows(
        jnp.stack([jnp.sum(query_pre * query_pre, axis=1), jnp.sum(key_pre * key_pre, axis=1)])
    )
    inverses = lax.rsqrt(squares / D + EPS)
    query_inv, key_inv = inverses[0][:, None], inverses[1][:, None]
    marks = jnp.stack([positions, block_ids])
    marks = by_side(marks, x_send(marks), 1)
    cosine, sine = rope_tables(marks[0].reshape(tokens))
    tile, token, common = attention_specs(length, heads)
    wide = jax.ShapeDtypeStruct((tokens, hw), BF)
    narrow = jax.ShapeDtypeStruct((heads, tokens, 1), F32)
    attention_args = (
        pre, pre, pre, inverses.T, query_g, key_g, cosine, sine,
        marks[1].reshape(tokens, 1), marks[1].reshape(2 * seqs, 1, length),
    )
    query_rot, key_rot, attended, log_total = pl.pallas_call(
        attend_kernel,
        grid=(2 * seqs, heads),
        out_shape=(wide, wide, wide, narrow),
        in_specs=common,
        out_specs=(tile, tile, tile, token),
        compiler_params=pltpu.CompilerParams(vmem_limit_bytes=32 << 20),
        name="attend",
    )(*attention_args)
    attn_rows = row_total(dot_nt(attended, out_w).astype(BF), seqs)
    attn_inv = lax.rsqrt(jnp.mean(attn_rows * attn_rows, axis=1, keepdims=True) + EPS)
    hidden_rows = own_tokens.astype(F32) + attn_rows * attn_inv * attn_g
    mid_full = spread(hidden_rows.astype(BF).reshape(inputs.shape))
    gate_pre = dot(mid_full, gate_w)
    up_pre = dot(mid_full, up_w)
    gate_sig = jax.nn.sigmoid(gate_pre)
    mixed = (gate_pre * gate_sig * up_pre).astype(BF)
    ffn_rows = row_total(dot_nt(mixed, down_w).astype(BF), seqs)
    ffn_inv = lax.rsqrt(jnp.mean(ffn_rows * ffn_rows, axis=1, keepdims=True) + EPS)
    output_rows = hidden_rows + ffn_rows * ffn_inv * ffn_g

    ffn_back = norm_back(ffn_rows, ffn_inv, ffn_g, cot_rows)
    ffn_gain_part = jnp.sum(cot_rows * ffn_rows * ffn_inv, axis=0)
    ffn_back_full = spread(ffn_back.astype(BF).reshape(inputs.shape))
    down_grad = reduce_grad(ffn_back_full, mixed)
    mixed_grad = dot(ffn_back_full, down_w)
    gate_low = (mixed_grad * up_pre * gate_sig * (1.0 + gate_pre * (1.0 - gate_sig))).astype(BF)
    up_low = (mixed_grad * gate_pre * gate_sig).astype(BF)
    gate_grad = reduce_grad(mid_full, gate_low)
    up_grad = reduce_grad(mid_full, up_low)
    mid_part = (dot_nt(gate_low, gate_w) + dot_nt(up_low, up_w)).astype(BF)
    hidden_grad = cot_rows + row_total(mid_part, seqs)
    attn_back = norm_back(attn_rows, attn_inv, attn_g, hidden_grad)
    attn_gain_part = jnp.sum(hidden_grad * attn_rows * attn_inv, axis=0)
    attn_back_full = spread(attn_back.astype(BF).reshape(inputs.shape))
    out_grad = reduce_grad(attn_back_full, attended)
    attended_grad = dot(attn_back_full, out_w).astype(BF)
    scaled_out = jax.ShapeDtypeStruct((tokens, hw), F32)
    gain_out = jax.ShapeDtypeStruct((2 * seqs, 1, hw), F32)
    gain_tile = pl.BlockSpec((1, 1, HD), lambda s, h: (s, 0, h))
    query_scaled, key_scaled, value_back, query_dots, key_dots, query_parts, key_parts = (
        pl.pallas_call(
            attend_back_kernel,
            grid=(2 * seqs, heads),
            out_shape=(scaled_out, scaled_out, wide, narrow, narrow, gain_out, gain_out),
            in_specs=common + [tile, tile, tile, token],
            out_specs=(tile, tile, tile, token, token, gain_tile, gain_tile),
            compiler_params=pltpu.CompilerParams(vmem_limit_bytes=32 << 20),
            name="attend_back",
        )(*attention_args, query_rot, key_rot, attended_grad, log_total)
    )
    query_gain_part = jnp.sum(query_parts, axis=(0, 1))
    key_gain_part = jnp.sum(key_parts, axis=(0, 1))
    dots = sum_rows(
        jnp.stack([jnp.sum(query_dots, axis=(0, 2)), jnp.sum(key_dots, axis=(0, 2))])
    )
    query_dot, key_dot = dots[0][:, None], dots[1][:, None]
    query_low = (query_inv * query_scaled - query_pre * query_inv**3 * (query_dot / D)).astype(BF)
    key_low = (key_inv * key_scaled - key_pre * key_inv**3 * (key_dot / D)).astype(BF)
    qkv_low = jnp.concatenate([query_low, key_low, value_back], axis=1)
    qkv_grad = reduce_grad(tok_full, qkv_low)
    input_rows = hidden_grad + row_total(dot_nt(qkv_low, qkv_w).astype(BF), seqs)

    def own_columns(grad):
        return by_side(grad[0], grad[1], 1).astype(F32)

    def own_thirds(grad, which):
        return own_columns([part[:, which * hw : (which + 1) * hw] for part in grad])

    def sum_dp(array):
        step = 1
        while step < dp:
            array = array + lax.ppermute(array, "dp", [(i, i ^ step) for i in range(dp)])
            step *= 2
        return array

    def placed(part):
        return lax.dynamic_update_slice(jnp.zeros((2 * hw,), F32), part, (side * hw,))

    shared = jnp.stack([attn_gain_part, ffn_gain_part])
    shared = shared + core_send(shared)
    shared = shared + y_send(shared)
    gains = sum_dp(
        jnp.concatenate(
            [placed(query_gain_part), placed(key_gain_part), shared.reshape(-1)]
        ).reshape(-1, HD)
    ).reshape(-1)
    return (
        output_rows.astype(BF).reshape(inputs.shape),
        input_rows.reshape(inputs.shape),
        own_thirds(qkv_grad, 0),
        own_thirds(qkv_grad, 1),
        own_thirds(qkv_grad, 2),
        own_columns(out_grad),
        gains[: 2 * hw],
        gains[2 * hw : 4 * hw],
        gains[4 * hw : 4 * hw + D],
        own_columns(gate_grad),
        own_columns(up_grad),
        own_columns(down_grad),
        gains[4 * hw + D :],
    )


def solution(mesh):
    whole = P()
    both = P("dp", "tensor")
    rows = P("dp", "tensor", None)
    lanes = P("tensor")
    return jax.shard_map(
        body,
        mesh=mesh,
        in_specs=(
            rows, both, both, both, both, lanes, lanes, whole, both, both, both, whole,
            P("dp", None), P("dp", None), rows,
        ),
        out_specs=(
            rows, rows, both, both, both, both, lanes, lanes, whole, both, both, both, whole,
        ),
        check_vma=False,
    )
```
